128 devices in a mesh: segment: 4 (over z), expert: 8 (over y, core), tensor: 4 (over x).
Axes of the slice: x: 4, y: 4, z: 4, core: 2. Of those that a mesh axis runs over, the one named last changes fastest.
Arguments:
- inputs: bfloat16 [2, 512, 3072], P(None, 'expert', 'tensor'), may hold values from -40 to 40
- norm_gain: float32 [4, 3072], P('segment', 'tensor'), may hold values from 0.5 to 1.5
- up_weight: bfloat16 [4, 8, 3072, 8192], P('segment', 'expert', None, 'tensor'), may hold values from -0.109375 to 0.109375
- down_weight: bfloat16 [4, 8, 8192, 3072], P('segment', 'expert', 'tensor'), may hold values from -0.0625 to 0.0625
- routing: int32 [4, 2, 512, 2], P('segment', None, 'expert'), may hold values from 0 to 7, all different within a row; in each aligned block of 64 rows (0 to 63, 64 to 127, ..., all dimensions but the last counted through in order) at most 32 rows name the same one
- gates: float32 [4, 2, 512, 2], P('segment', None, 'expert'), may hold values from 0.2 to 1
Outputs:
- segment_out: bfloat16 [4, 2, 512, 3072], P('segment', None, 'expert', 'tensor')
The draws below stay inside these ranges and needn't reach their ends.
Inputs may be any that keep to these rules, and one draw needn't show every extreme that they name: `routing`: in each aligned block of 64 rows of one segment and micro-batch (the rows of one index of the expert axis) no expert is named by more than 32 rows, a bound that some block reaches; the 2 experts of a row differ.
All inputs are finite; a program needn't handle non-finite values.
Results may differ from the reference program's by a relative error of at most 0.013.
Values may be sent and summed in bfloat16 or wider, within the bound.
A program may use at most 128 MiB of HBM per device.

```python
import math
import jax
import jax.numpy as jnp
import numpy as np
from jax import lax

D = 3072
FF = 8192
TOP = 2
MB = 2
TOK_DEV = 64
EXPERTS = 8
TOKENS = 512
CAP = 32
SEGMENTS = 4
FF_GROUPS = 4


def draw_inputs(key, part):
    key_base, key_rows = jax.random.split(jax.random.fold_in(key, 11))
    column_scale = 0.25 * 10.0 ** (jnp.arange(D, dtype=jnp.float32) / D)
    row_scale = jnp.exp(jax.random.uniform(key_rows, (MB, TOKENS, 1), jnp.float32, math.log(0.4), math.log(4.0)))
    base = jnp.clip(jax.random.normal(key_base, (MB, TOKENS, D), jnp.float32), -4.0, 4.0)
    return (base * row_scale * column_scale[None, None, :]).astype(jnp.bfloat16)


def level_of(own_key, dims, cuts, smallest, top_value):
    def one(dim, parts):
        steps = jax.random.uniform(jax.random.fold_in(jax.random.fold_in(own_key, 6), dim), (parts,), jnp.float32, smallest / len(cuts), top_value / len(cuts))
        return jnp.repeat(jnp.exp(steps), dims[dim] // parts).reshape((-1,) + (1,) * (len(dims) - dim - 1))

    gain = one(*cuts[0])
    for cut in cuts[1:]:
        gain = gain * one(*cut)
    return gain


def assign_block(rng, own, number, rows, count, top, reach, lean):
    order = jax.random.permutation(rng, count)
    packed, common = portions_of(count, rows * top, reach, lean, True), portions_of(count, rows * top, reach, lean, False)
    places = jnp.arange(count)

    def named(sizes, rotation):
        used = int((sizes > 0).sum())
        fixed = max(1, used // 4)
        shifted = fixed + (places - fixed + rotation * (used - fixed)) % max(1, count - fixed)
        return jnp.zeros((count,), jnp.int32).at[order[jnp.where(places < fixed, places, shifted)]].set(jnp.asarray(sizes, jnp.int32))

    sizes = jnp.where(number % 4 == 0, named(packed, number // 4), named(common, number - number // 4 - 1))
    mixed = jax.random.permutation(jax.random.fold_in(own, 3), count)
    giver, receiver = mixed[0:count // 2 * 2:2], mixed[1:count // 2 * 2:2]
    margin = jnp.minimum(sizes[giver] - 1, reach - sizes[receiver]) // 2
    margin = jnp.where((giver == order[0]) | (receiver == order[0]) | (sizes[receiver] == 0), 0, jnp.maximum(margin, 0))
    shifted = jax.random.randint(jax.random.fold_in(own, 4), (count // 2,), 0, 1 << 20) % (margin + 1)
    sizes = sizes.at[giver].add(-shifted).at[receiver].add(shifted)
    items = jnp.searchsorted(jnp.cumsum(sizes), jnp.arange(rows * top), side="right").astype(jnp.int32)
    listing = items.reshape(top, rows).T
    listing = listing[jax.random.permutation(jax.random.fold_in(own, 1), rows)]
    rotation = jax.random.randint(jax.random.fold_in(own, 2), (rows, 1), 0, top)
    return jnp.take_along_axis(listing, (jnp.arange(top)[None, :] + rotation) % top, axis=1)


def portions_of(number_of, total, bound, skew, full):
    weights = [(1 << 20) // math.isqrt(grade ** skew) + 1 for grade in range(1, number_of + 1)]
    largest = bound if full else min(bound, max(-(-total // number_of), total * weights[0] // sum(weights)))
    least = 1 if total - largest >= number_of - 1 else 0
    given, spare = [largest] + [least] * (number_of - 1), total - largest - least * (number_of - 1)
    while spare > 0:
        free = [i for i in range(1, number_of) if given[i] < largest] or [i for i in range(1, number_of) if given[i] < bound]
        whole, remaining = sum([weights[i] for i in free]), spare
        for i in free:
            extra = min(bound - given[i], max(1, remaining * weights[i] // whole), spare)
            given[i] = given[i] + extra
            spare = spare - extra
    return np.array(given)


def noise(own_key, dims, scale, bound, cuts=(), kind=jnp.bfloat16):
    gain = level_of(own_key, dims, cuts, -0.22, 0.18) if cuts else 1.0
    values = jax.random.normal(own_key, dims, jnp.float32) * scale * gain
    return jnp.minimum(jnp.maximum(values, -bound), bound).astype(kind)


def setup_inputs(seed: int = 0) -> dict:
    arg_keys = jax.random.split(jax.random.key(seed), 7)
    inputs = draw_inputs(jax.random.fold_in(arg_keys[6], 71), 0)
    norm_gain = jnp.clip(0.5 + 1.0 * jax.random.uniform(arg_keys[1], (SEGMENTS, D), jnp.float32) ** level_of(arg_keys[1], (SEGMENTS, D), ((0, 4), (1, 4)), -0.2, 0.2), 0.5, 1.5)
    up_weight = noise(arg_keys[2], (SEGMENTS, EXPERTS, D, FF), D ** -0.5, 0.109375, ((0, 4), (1, 8), (3, 4)))
    down_weight = noise(arg_keys[3], (SEGMENTS, EXPERTS, FF, D), FF ** -0.5, 0.0625, ((0, 4), (1, 8), (2, 4)))
    routing_keys = jax.random.split(jax.random.fold_in(arg_keys[4], 1), SEGMENTS * MB * TOKENS // TOK_DEV)
    routing_turns = jax.random.permutation(jax.random.fold_in(arg_keys[4], 3), SEGMENTS * MB * TOKENS // TOK_DEV)
    routing = jax.vmap(lambda own, number: assign_block(jax.random.fold_in(arg_keys[4], 2), own, number, TOK_DEV, EXPERTS, TOP, CAP, 2))(routing_keys, routing_turns).reshape((SEGMENTS, MB, TOKENS, TOP))
    gates = jnp.clip(jnp.exp(math.log(1.0) - 1.609438 * jax.random.uniform(arg_keys[5], (SEGMENTS, MB, TOKENS, TOP), jnp.float32) ** level_of(arg_keys[5], (SEGMENTS, MB, TOKENS, TOP), ((0, 4), (2, 8)), -0.2, 0.2)), 0.2, 1.0)
    return {"inputs": inputs, "norm_gain": norm_gain, "up_weight": up_weight, "down_weight": down_weight, "routing": routing, "gates": gates}


def slot_numbers(choices, expert_count):
    flat_ids = choices.reshape(-1)
    onehot = (flat_ids[:, None] == jnp.arange(expert_count, dtype=jnp.int32)[None, :]).astype(jnp.int32)
    earlier = (jnp.cumsum(onehot, axis=0) - onehot).astype(jnp.int32)
    return lax.optimization_barrier(jnp.sum(earlier * onehot, axis=1)).astype(jnp.int32)

def segment_section(stream, gain_row, up_mats, down_mats, choices, weights):
    stream_f = stream.astype(jnp.float32)
    mean_sq = lax.optimization_barrier(jnp.mean(stream_f * stream_f, axis=1, keepdims=True))
    normed = (stream_f * lax.rsqrt(mean_sq + 1e-05) * gain_row).astype(jnp.bfloat16)
    blocks = TOKENS // TOK_DEV
    per_expert = blocks * CAP
    slot_ids = jax.vmap(lambda block_ids: slot_numbers(block_ids, EXPERTS))(choices.reshape(blocks, TOK_DEV, TOP)).reshape(TOKENS, TOP)
    block_of = (jnp.arange(TOKENS, dtype=jnp.int32) // TOK_DEV)[:, None]
    position = (choices * per_expert + block_of * CAP + slot_ids).astype(jnp.int32)
    buffer = jnp.zeros((EXPERTS * per_expert, D), jnp.bfloat16)
    buffer = buffer.at[position.reshape(-1)].set(jnp.repeat(normed, TOP, axis=0))
    buffer = buffer.reshape(EXPERTS, per_expert, D)
    group_width = FF // FF_GROUPS

    def one_expert(operands):
        rows_in, up_mat, down_mat = operands
        hidden = jax.nn.silu(jnp.dot(rows_in, up_mat, preferred_element_type=jnp.float32)).astype(jnp.bfloat16)
        summed = jnp.zeros((per_expert, D), jnp.float32)
        for group_index in range(FF_GROUPS):
            lower = group_index * group_width
            partial_value = jnp.dot(hidden[:, lower:lower + group_width], down_mat[lower:lower + group_width], preferred_element_type=jnp.float32).astype(jnp.bfloat16)
            summed = summed + lax.optimization_barrier(partial_value).astype(jnp.float32)
        return summed
    expert_out = lax.map(one_expert, (buffer, up_mats, down_mats)).reshape(EXPERTS * per_expert, D)
    picked = expert_out[position]
    updated = stream_f + lax.optimization_barrier(jnp.sum(weights[:, :, None] * picked, axis=1))
    return updated.astype(jnp.bfloat16)

def reference(inputs, norm_gain, up_weight, down_weight, routing, gates):
    results = []
    for batch_index in range(MB):
        stream = inputs[batch_index]
        per_segment = []
        for segment_index in range(SEGMENTS):
            stream = segment_section(stream, norm_gain[segment_index], up_weight[segment_index], down_weight[segment_index], routing[segment_index, batch_index], gates[segment_index, batch_index])
            per_segment.append(stream)
        results.append(jnp.stack(per_segment))
    return jnp.stack(results, axis=1)
```

```python
import functools

import jax
import jax.numpy as jnp
from jax import lax
from jax.experimental import pallas as pl
from jax.experimental.pallas import tpu as pltpu
from jax.sharding import PartitionSpec as P

MESH = pl.DeviceIdType.MESH
RING = 4
CAP = 32
F32 = jnp.float32
BF16 = jnp.bfloat16


def relay_kernel(
    inp, meta, gain, up_hbm, down_hbm, out,
    wup, wdn, xbuf, obuf, pbuf, r1, r2, r3, r4, res, xg, hid, dmat, pmat, gslot, mbuf, gbuf, chosen,
    w_sem, m_send, m_recv, n_send, n_recv, z_send, z_recv,
    gf_recv, gg_recv, gp_recv, g_send, sp_recv, s1_recv, s2_recv, s3_recv, s4_recv, s_send,
):
    s = lax.axis_index("segment")
    e = lax.axis_index("expert")
    t = lax.axis_index("tensor")
    segments = lax.axis_size("segment")
    rows, quarter = inp.shape[1], inp.shape[2]
    half = rows // 2
    width = quarter * RING
    hidden = wup.shape[1]
    batches = inp.shape[0]
    y = e // 2
    c = e - 2 * y
    f = t * (1 - c) + y * c
    g = y * (1 - c) + t * c

    def mod4(v):
        return lax.rem(v + 8, 4)

    def device(df, dg):
        nf, ng = mod4(f + df), mod4(g + dg)
        nt = nf * (1 - c) + ng * c
        ny = ng * (1 - c) + nf * c
        return {"tensor": nt, "expert": 2 * ny + c}

    partner = {"expert": 2 * y + (1 - c)}
    above = {"segment": lax.rem(s + 1, segments)}
    below = {"segment": lax.rem(s + segments - 1, segments)}

    def place(gi, fi):
        q = fi * (1 - c) + gi * c
        yy = gi * (1 - c) + fi * c
        return q * RING + yy

    def send(src, dst, send_sem, recv_sem, where):
        pltpu.make_async_remote_copy(
            src_ref=src, dst_ref=dst, send_sem=send_sem, recv_sem=recv_sem, device_id=where, device_id_type=MESH
        ).start()

    def arrive(ref, sem):
        pltpu.make_async_copy(ref, ref, sem).wait()

    up_copy = pltpu.make_async_copy(up_hbm, wup, w_sem.at[0])
    down_copy = pltpu.make_async_copy(down_hbm, wdn, w_sem.at[1])
    up_copy.start()
    down_copy.start()

    barrier = pltpu.get_barrier_semaphore()
    for step in range(1, 8):
        pl.semaphore_signal(barrier, inc=1, device_id={"expert": lax.rem(e + step, 8)}, device_id_type=MESH)
    for step in range(1, RING):
        pl.semaphore_signal(barrier, inc=1, device_id={"tensor": lax.rem(t + step, RING)}, device_id_type=MESH)
    pl.semaphore_signal(barrier, inc=1, device_id=above, device_id_type=MESH)
    pl.semaphore_signal(barrier, inc=1, device_id=below, device_id_type=MESH)
    pl.semaphore_wait(barrier, 12)

    @pl.when(s == 0)
    def _():
        for m in range(batches):
            pltpu.make_async_copy(inp.at[m], xbuf.at[(m * 2 + c) * 16 + place(g, f)], z_recv.at[m]).start()

    for step in range(1, 8):
        send(meta, mbuf.at[e], m_send.at[step - 1], m_recv.at[step - 1], {"expert": lax.rem(e + step, 8)})
    for step in range(1, RING):
        send(gain, gbuf.at[t], n_send.at[step - 1], n_recv.at[step - 1], {"tensor": lax.rem(t + step, RING)})
    own_meta = pltpu.make_async_copy(meta, mbuf.at[e], m_send.at[7])
    own_gain = pltpu.make_async_copy(gain, gbuf.at[t], n_send.at[3])
    own_meta.start()
    own_gain.start()

    def gather_first(m):
        base = (m * 2 + c) * 16
        full = lambda fi: xbuf.at[base + place(g, fi)]
        lower = lambda fi: xbuf.at[base + place(g, fi), pl.ds(0, half)]
        upper = lambda fi: xbuf.at[base + place(g, fi), pl.ds(half, half)]
        f_up, f_dn, f_far = mod4(f + 1), mod4(f - 1), mod4(f + 2)
        order = (f, f_dn, f_up, f_far)
        arrive(full(f), z_recv.at[m])
        send(full(f), full(f), g_send.at[m], gf_recv.at[m, 0], device(1, 0))
        send(full(f), full(f), g_send.at[m], gf_recv.at[m, 1], device(-1, 0))

        def spread(fi, number):
            ref = full(fi)
            send(ref, ref, g_send.at[m], gg_recv.at[m, number, 0], device(0, 1))
            send(ref, ref, g_send.at[m], gg_recv.at[m, number, 1], device(0, -1))
            send(ref, ref, g_send.at[m], gp_recv.at[m], partner)

        spread(f, 0)
        arrive(full(f_dn), gf_recv.at[m, 0])
        send(lower(f_dn), lower(f_dn), g_send.at[m], gf_recv.at[m, 2], device(1, 0))
        spread(f_dn, 1)
        arrive(full(f_up), gf_recv.at[m, 1])
        send(upper(f_up), upper(f_up), g_send.at[m], gf_recv.at[m, 3], device(-1, 0))
        spread(f_up, 2)
        arrive(lower(f_far), gf_recv.at[m, 2])
        arrive(upper(f_far), gf_recv.at[m, 3])
        spread(f_far, 3)

        for number, fi in enumerate(order):
            from_dn = lambda gi: xbuf.at[base + place(gi, fi)]
            ref = from_dn(mod4(g - 1))
            arrive(ref, gg_recv.at[m, number, 0])
            part = xbuf.at[base + place(mod4(g - 1), fi), pl.ds(0, half)]
            send(part, part, g_send.at[m], gg_recv.at[m, number, 2], device(0, 1))
            send(ref, ref, g_send.at[m], gp_recv.at[m], partner)
            ref = from_dn(mod4(g + 1))
            arrive(ref, gg_recv.at[m, number, 1])
            part = xbuf.at[base + place(mod4(g + 1), fi), pl.ds(half, half)]
            send(part, part, g_send.at[m], gg_recv.at[m, number, 3], device(0, -1))
            send(ref, ref, g_send.at[m], gp_recv.at[m], partner)
        for number, fi in enumerate(order):
            spot = base + place(mod4(g + 2), fi)
            arrive(xbuf.at[spot, pl.ds(0, half)], gg_recv.at[m, number, 2])
            arrive(xbuf.at[spot, pl.ds(half, half)], gg_recv.at[m, number, 3])
            send(xbuf.at[spot], xbuf.at[spot], g_send.at[m], gp_recv.at[m], partner)
        arrive(xbuf.at[pl.ds((m * 2 + 1 - c) * 16, 16)], gp_recv.at[m])

    def set_up_routing(m):
        slots = RING * CAP
        tokens = RING * rows
        mine = e.astype(F32)
        row_i = lax.broadcasted_iota(jnp.int32, (tokens, tokens), 0)
        col_i = lax.broadcasted_iota(jnp.int32, (tokens, tokens), 1)
        earlier = ((row_i < col_i) & (row_i // rows == col_i // rows)).astype(BF16)
        slot_id = lax.broadcasted_iota(jnp.int32, (slots, tokens), 0).astype(F32)
        first_slot = (lax.broadcasted_iota(jnp.int32, (1, tokens), 1) // rows * CAP).astype(F32)
        for p in range(2):
            table = jnp.concatenate([mbuf[p] + mbuf[2 + p], mbuf[4 + p] + mbuf[6 + p]], axis=1)
            for mb in range(batches):
                hit0 = table[2 * mb:2 * mb + 1] == mine
                hit1 = table[2 * mb + 1:2 * mb + 2] == mine
                named = jnp.where(hit0 | hit1, 1.0, 0.0)
                chosen[...] = jnp.broadcast_to(named, chosen.shape).astype(BF16)
                before = jnp.dot(chosen[...], earlier, preferred_element_type=F32)[0:1]
                position = jnp.where(named > 0.0, before + first_slot, -1.0)
                gate = jnp.where(hit0, table[4 + 2 * mb:5 + 2 * mb], 0.0) + jnp.where(
                    hit1, table[5 + 2 * mb:6 + 2 * mb], 0.0
                )
                onehot = jnp.where(slot_id == position, 1.0, 0.0)
                dmat[mb, p] = onehot.astype(BF16)
                pmat[mb, p] = onehot.T.astype(BF16)
                gslot[mb, pl.ds(p * slots, slots)] = jnp.sum(onehot * gate, axis=1, keepdims=True)

    def experts(m):
        slots = RING * CAP
        total = [jnp.zeros((slots, 1), F32) for _ in range(2)]
        for q in range(RING):
            for p in range(2):
                tokens = xbuf[pl.ds((m * 2 + p) * 16 + q * RING, RING)].reshape(RING * rows, quarter)
                picked = jnp.dot(dmat[m, p], tokens, preferred_element_type=F32)
                total[p] += jnp.sum(picked * picked, axis=1, keepdims=True)
                xg[p * slots:(p + 1) * slots, q * quarter:(q + 1) * quarter] = (picked * gbuf[q, 0:1]).astype(BF16)
        scale = lax.rsqrt(jnp.concatenate(total, axis=0) / width + 1e-05)
        weight = gslot[m]
        step = hidden // 4

        def up(i, carry):
            cols = pl.ds(pl.multiple_of(i * step, step), step)
            v = jnp.dot(xg[...], wup[:, cols], preferred_element_type=F32) * scale
            hid[:, cols] = (v / (1.0 + jnp.exp(-v)) * weight).astype(BF16)
            return carry

        lax.fori_loop(0, 4, up, 0)

    def chunk(number):
        return mod4(t + (2, -1, 1, 0)[number])

    def down(m, number):
        slots = RING * CAP
        q = chunk(number)
        cols = pl.ds(pl.multiple_of(q * quarter, quarter), quarter)
        part = jnp.dot(hid[...], wdn[:, cols], preferred_element_type=F32).astype(BF16)
        for p in range(2):
            value = jnp.dot(pmat[m, p], part[p * slots:(p + 1) * slots], preferred_element_type=F32)
            obuf[pl.ds(p * 16 + q * RING, RING)] = value.astype(BF16).reshape(RING, rows, quarter)
        send(
            obuf.at[pl.ds((1 - c) * 16 + q * RING, RING)], pbuf.at[m, pl.ds(q * RING, RING)],
            s_send.at[m], sp_recv.at[m, number], partner,
        )

    def join(m, number):
        q = chunk(number)
        arrive(pbuf.at[m, pl.ds(q * RING, RING)], sp_recv.at[m, number])
        mine = pl.ds(c * 16 + q * RING, RING)
        obuf[mine] = (obuf[mine].astype(F32) + pbuf[m, pl.ds(q * RING, RING)].astype(F32)).astype(BF16)

    def scatter(m):
        own = c * 16
        f_far, f_dn, f_up = mod4(f + 2), mod4(f - 1), mod4(f + 1)
        order = (f_far, f_dn, f_up, f)
        low, high = pl.ds(0, half), pl.ds(half, half)
        for number, fi in enumerate(order):
            spot = own + place(mod4(g + 2), fi)
            send(obuf.at[spot, low], r1.at[m, 0, number], s_send.at[m], s1_recv.at[m, number, 0], device(0, 1))
            send(obuf.at[spot, high], r1.at[m, 1, number], s_send.at[m], s1_recv.at[m, number, 1], device(0, -1))
        for number, fi in enumerate(order):
            for side, dg, part in ((0, 1, low), (1, -1, high)):
                spot = own + place(mod4(g + dg), fi)
                arrive(r1.at[m, side, number], s1_recv.at[m, number, side])
                obuf[spot, part] = (obuf[spot, part].astype(F32) + r1[m, side, number].astype(F32)).astype(BF16)
                send(obuf.at[spot], r2.at[m, side, number], s_send.at[m], s2_recv.at[m, number, side], device(0, dg))
        for number, fi in enumerate(order):
            spot = own + place(g, fi)
            arrive(r2.at[m, 0, number], s2_recv.at[m, number, 0])
            arrive(r2.at[m, 1, number], s2_recv.at[m, number, 1])
            if number in (1, 2):
                side, df, part = ((1, -1, high), (0, 1, low))[number - 1]
            total = obuf[spot].astype(F32) + r2[m, 0, number].astype(F32) + r2[m, 1, number].astype(F32)
            if number == 0:
                obuf[spot] = total.astype(BF16)
                send(obuf.at[spot, low], r3.at[m, 0], s_send.at[m], s3_recv.at[m, 0], device(1, 0))
                send(obuf.at[spot, high], r3.at[m, 1], s_send.at[m], s3_recv.at[m, 1], device(-1, 0))
            elif number == 3:
                final = total
            else:
                obuf[spot] = total.astype(BF16)
                arrive(r3.at[m, side], s3_recv.at[m, side])
                obuf[spot, part] = (obuf[spot, part].astype(F32) + r3[m, side].astype(F32)).astype(BF16)
                send(obuf.at[spot], r4.at[m, side], s_send.at[m], s4_recv.at[m, side], device(df, 0))
        arrive(r4.at[m, 0], s4_recv.at[m, 0])
        arrive(r4.at[m, 1], s4_recv.at[m, 1])
        stream = xbuf[(m * 2 + c) * 16 + place(g, f)].astype(F32)
        result = (stream + (final + r4[m, 0].astype(F32) + r4[m, 1].astype(F32))).astype(BF16)
        res[m] = result
        out[m] = result

        @pl.when(s < segments - 1)
        def _():
            send(res.at[m], xbuf.at[(m * 2 + c) * 16 + place(g, f)], z_send.at[m], z_recv.at[m], above)

    def one_batch(m, carry):
        gather_first(m)

        @pl.when(m == 0)
        def _():
            for step in range(7):
                arrive(meta, m_recv.at[step])
            for step in range(3):
                arrive(gain, n_recv.at[step])
            own_meta.wait()
            own_gain.wait()
            set_up_routing(m)
            up_copy.wait()
            down_copy.wait()

        experts(m)
        for number in range(RING):
            down(m, number)
        for number in range(RING):
            join(m, number)
        scatter(m)
        arrive(xbuf.at[pl.ds(0, 31)], g_send.at[m])
        arrive(xbuf.at[pl.ds(0, 31)], s_send.at[m])
        return carry

    lax.fori_loop(0, batches, one_batch, 0)

    for step in range(7):
        arrive(meta, m_send.at[step])
    for step in range(3):
        arrive(gain, n_send.at[step])

    @pl.when(s < segments - 1)
    def _():
        for m in range(batches):
            arrive(res.at[m], z_send.at[m])


def on_device(inputs, norm_gain, up_weight, down_weight, routing, gates):
    batches, rows, quarter = inputs.shape
    width, hidden = up_weight.shape[2:]
    lanes = 2 * rows
    choice_rows = routing[0].astype(F32).transpose(0, 2, 1).reshape(2 * batches, rows)
    gate_rows = gates[0].transpose(0, 2, 1).reshape(2 * batches, rows)
    both = jnp.concatenate([choice_rows, gate_rows], axis=0)
    place = lax.rem(lax.axis_index("expert") // 2, 2)
    filled = jnp.concatenate([both, both], axis=1)
    meta = jnp.where(jnp.arange(lanes)[None, :] // rows == place, filled, 0.0)
    gain = jnp.broadcast_to(norm_gain, (8, quarter))
    slots = RING * CAP
    half = rows // 2
    dma = pltpu.SemaphoreType.DMA
    vmem = pl.BlockSpec(memory_space=pltpu.VMEM)
    hbm = pl.BlockSpec(memory_space=pl.ANY)
    result = pl.pallas_call(
        relay_kernel,
        out_shape=jax.ShapeDtypeStruct((batches, rows, quarter), BF16),
        in_specs=[vmem, vmem, vmem, hbm, hbm],
        out_specs=vmem,
        scratch_shapes=[
            pltpu.VMEM((width, hidden), BF16),
            pltpu.VMEM((hidden, width), BF16),
            pltpu.VMEM((batches * 2 * 16, rows, quarter), BF16),
            pltpu.VMEM((2 * 16, rows, quarter), BF16),
            pltpu.VMEM((batches, 16, rows, quarter), BF16),
            pltpu.VMEM((batches, 2, RING, half, quarter), BF16),
            pltpu.VMEM((batches, 2, RING, rows, quarter), BF16),
            pltpu.VMEM((batches, 2, half, quarter), BF16),
            pltpu.VMEM((batches, 2, rows, quarter), BF16),
            pltpu.VMEM((batches, rows, quarter), BF16),
            pltpu.VMEM((2 * slots, width), BF16),
            pltpu.VMEM((2 * slots, hidden), BF16),
            pltpu.VMEM((batches, 2, slots, RING * rows), BF16),
            pltpu.VMEM((batches, 2, RING * rows, slots), BF16),
            pltpu.VMEM((batches, 2 * slots, 1), F32),
            pltpu.VMEM((8, 8, lanes), F32),
            pltpu.VMEM((RING, 8, quarter), F32),
            pltpu.VMEM((16, RING * rows), BF16),
            dma((2,)),
            dma((8,)),
            dma((7,)),
            dma((4,)),
            dma((3,)),
            dma((batches,)),
            dma((batches,)),
            dma((batches, 4)),
            dma((batches, RING, 4)),
            dma((batches,)),
            dma((batches,)),
            dma((batches, RING)),
            dma((batches, RING, 2)),
            dma((batches, RING, 2)),
            dma((batches, 2)),
            dma((batches, 2)),
            dma((batches,)),
        ],
        compiler_params=pltpu.CompilerParams(
            collective_id=0, has_side_effects=True, vmem_limit_bytes=67043328
        ),
    )(inputs, meta, gain, up_weight.reshape(width, hidden), down_weight.reshape(hidden, width))
    return result[None]


def solution(mesh):
    return jax.shard_map(
        on_device,
        mesh=mesh,
        in_specs=(
            P(None, "expert", "tensor"),
            P("segment", "tensor"),
            P("segment", "expert", None, "tensor"),
            P("segment", "expert", "tensor", None),
            P("segment", None, "expert", None),
            P("segment", None, "expert", None),
        ),
        out_specs=P("segment", None, "expert", "tensor"),
        check_vma=False,
    )
```

```python
import functools

import jax
import jax.numpy as jnp
from jax import lax
from jax.experimental import pallas as pl
from jax.experimental.pallas import tpu as pltpu
from jax.sharding import PartitionSpec as P

MESH = pl.DeviceIdType.MESH
RING = 4
CAP = 32
F32 = jnp.float32
BF16 = jnp.bfloat16


def relay_kernel(
    inp, meta, gain, up_hbm, down_hbm, out,
    wup, wdn, xbuf, obuf, pbuf, r2, r3, res, xg, acc, squares, hid, dmat, pmat, gslot, mbuf, gbuf, chosen,
    w_sem, m_send, m_recv, n_send, n_recv, z_send, z_recv,
    gf_recv, gg_recv, gp_recv, f_send, g_send, sp_recv, s2_recv, s3_recv, s_send,
):
    s = lax.axis_index("segment")
    e = lax.axis_index("expert")
    t = lax.axis_index("tensor")
    segments = lax.axis_size("segment")
    rows, quarter = inp.shape[1], inp.shape[2]
    width = quarter * RING
    hidden = wup.shape[1]
    batches = inp.shape[0]
    y = e // 2
    c = e - 2 * y
    f = t * (1 - c) + y * c
    g = y * (1 - c) + t * c

    def part(h):
        return pl.ds(h * (rows // 2), rows // 2)

    def mod4(v):
        return lax.rem(v + 8, 4)

    def device(df, dg):
        nf, ng = mod4(f + df), mod4(g + dg)
        nt = nf * (1 - c) + ng * c
        ny = ng * (1 - c) + nf * c
        return {"tensor": nt, "expert": 2 * ny + c}

    partner = {"expert": 2 * y + (1 - c)}
    above = {"segment": lax.rem(s + 1, segments)}
    below = {"segment": lax.rem(s + segments - 1, segments)}

    def place(gi, fi):
        q = fi * (1 - c) + gi * c
        yy = gi * (1 - c) + fi * c
        return q * RING + yy

    def send(src, dst, send_sem, recv_sem, where):
        pltpu.make_async_remote_copy(
            src_ref=src, dst_ref=dst, send_sem=send_sem, recv_sem=recv_sem, device_id=where, device_id_type=MESH
        ).start()

    def arrive(ref, sem):
        pltpu.make_async_copy(ref, ref, sem).wait()

    up_copy = pltpu.make_async_copy(up_hbm, wup, w_sem.at[0])
    down_copy = pltpu.make_async_copy(down_hbm, wdn, w_sem.at[1])
    up_copy.start()

    barrier = pltpu.get_barrier_semaphore()
    for step in range(1, 8):
        pl.semaphore_signal(barrier, inc=1, device_id={"expert": lax.rem(e + step, 8)}, device_id_type=MESH)
    for step in range(1, RING):
        pl.semaphore_signal(barrier, inc=1, device_id={"tensor": lax.rem(t + step, RING)}, device_id_type=MESH)
    pl.semaphore_signal(barrier, inc=1, device_id=above, device_id_type=MESH)
    pl.semaphore_signal(barrier, inc=1, device_id=below, device_id_type=MESH)
    pl.semaphore_wait(barrier, 12)
    down_copy.start()

    @pl.when(s == 0)
    def _():
        for m in range(batches):
            for h in range(2):
                here = xbuf.at[(m * 2 + c) * 16 + place(g, f), part(h)]
                pltpu.make_async_copy(inp.at[m, part(h)], here, z_recv.at[m, h]).start()

    for step in range(1, 8):
        send(meta, mbuf.at[e], m_send.at[step - 1], m_recv.at[step - 1], {"expert": lax.rem(e + step, 8)})
    for step in range(1, RING):
        send(gain, gbuf.at[t], n_send.at[step - 1], n_recv.at[step - 1], {"tensor": lax.rem(t + step, RING)})
    own_meta = pltpu.make_async_copy(meta, mbuf.at[e], m_send.at[7])
    own_gain = pltpu.make_async_copy(gain, gbuf.at[t], n_send.at[3])
    own_meta.start()
    own_gain.start()

    slots = RING * CAP
    tokens = RING * rows
    f_far, f_dn, f_up = mod4(f + 2), mod4(f - 1), mod4(f + 1)
    g_far, g_dn, g_up = mod4(g + 2), mod4(g - 1), mod4(g + 1)

    def gather_steps(m):
        base = (m * 2 + c) * 16
        order = (f, f_dn, f_up, f_far)

        def to_partner(ref, number, g_number):
            group = number * (1 - c) + g_number * c
            send(ref, ref, g_send.at[m], gp_recv.at[m, group], partner)

        def spread(number):
            ref = xbuf.at[base + place(g, order[number])]
            for kind, dg in enumerate((1, -1, 2)):
                send(ref, ref, g_send.at[m], gg_recv.at[m, number, kind], device(0, dg))
            to_partner(ref, number, 0)

        def pass_on(number, kinds=(0, 1, 2)):
            for kind in kinds:
                ref = xbuf.at[base + place((g_dn, g_up, g_far)[kind], order[number])]
                arrive(ref, gg_recv.at[m, number, kind])
                to_partner(ref, number, 1 + kind)

        def start():
            for h in range(2):
                own = xbuf.at[base + place(g, f), part(h)]
                arrive(own, z_recv.at[m, h])
                for kind, df in ((2, 2), (0, 1), (1, -1)):
                    send(own, own, f_send.at[m], gf_recv.at[m, kind, h], device(df, 0))
            arrive(xbuf.at[pl.ds(0, 3)], f_send.at[m])
            spread(0)

        def turn():
            for number, fi in ((1, f_dn), (2, f_up), (3, f_far)):
                for h in range(2):
                    arrive(xbuf.at[base + place(g, fi), part(h)], gf_recv.at[m, number - 1, h])
                spread(number)

        return start, turn, pass_on

    def set_up_routing():
        for step in range(7):
            arrive(meta, m_recv.at[step])
        for step in range(3):
            arrive(gain, n_recv.at[step])
        own_meta.wait()
        own_gain.wait()
        mine = e.astype(F32)
        row_i = lax.broadcasted_iota(jnp.int32, (tokens, tokens), 0)
        col_i = lax.broadcasted_iota(jnp.int32, (tokens, tokens), 1)
        earlier = ((row_i < col_i) & (row_i // rows == col_i // rows)).astype(BF16)
        slot_id = lax.broadcasted_iota(jnp.int32, (slots, tokens), 0).astype(F32)
        first_slot = (lax.broadcasted_iota(jnp.int32, (1, tokens), 1) // rows * CAP).astype(F32)
        for p in range(2):
            table = jnp.concatenate([mbuf[p] + mbuf[2 + p], mbuf[4 + p] + mbuf[6 + p]], axis=1)
            for mb in range(batches):
                hit0 = table[2 * mb:2 * mb + 1] == mine
                hit1 = table[2 * mb + 1:2 * mb + 2] == mine
                named = jnp.where(hit0 | hit1, 1.0, 0.0)
                chosen[...] = jnp.broadcast_to(named, chosen.shape).astype(BF16)
                before = jnp.dot(chosen[...], earlier, preferred_element_type=F32)[0:1]
                position = jnp.where(named > 0.0, before + first_slot, -1.0)
                gate = jnp.where(hit0, table[4 + 2 * mb:5 + 2 * mb], 0.0) + jnp.where(
                    hit1, table[5 + 2 * mb:6 + 2 * mb], 0.0
                )
                onehot = jnp.where(slot_id == position, 1.0, 0.0)
                dmat[mb, p] = onehot.astype(BF16)
                pmat[mb, p] = onehot.T.astype(BF16)
                gslot[mb, pl.ds(p * slots, slots)] = jnp.sum(onehot * gate, axis=1, keepdims=True)

    def up(m, number):
        q = mod4(t + (0, -1, 1, 2)[number])
        theirs = xbuf.at[pl.ds((m * 2 + 1 - c) * 16 + q * RING, RING)]
        arrive(theirs, gp_recv.at[m, number])
        for p in range(2):
            block = xbuf[pl.ds((m * 2 + p) * 16 + q * RING, RING)].reshape(tokens, quarter)
            picked = jnp.dot(dmat[m, p], block, preferred_element_type=F32)
            square = jnp.sum(picked * picked, axis=1, keepdims=True)
            mine = pl.ds(p * slots, slots)
            squares[mine] = square if number == 0 else squares[mine] + square
            xg[mine] = (picked * gbuf[q, 0:1]).astype(BF16)
        step = hidden // 2
        deep = pl.ds(pl.multiple_of(q * quarter, quarter), quarter)
        for i in range(2):
            cols = pl.ds(i * step, step)
            v = jnp.dot(xg[...], wup[deep, cols], preferred_element_type=F32)
            if number > 0:
                v = v + acc[:, cols]
            if number < RING - 1:
                acc[:, cols] = v
            else:
                v = v * lax.rsqrt(squares[...] / width + 1e-05)
                hid[:, cols] = (v / (1.0 + jnp.exp(-v)) * gslot[m]).astype(BF16)

    def chunk(number):
        return mod4(t + (2, -1, 1, 0)[number])

    def down(m, number):
        q = chunk(number)
        cols = pl.ds(pl.multiple_of(q * quarter, quarter), quarter)
        part = jnp.dot(hid[...], wdn[:, cols], preferred_element_type=F32).astype(BF16)
        for p in range(2):
            value = jnp.dot(pmat[m, p], part[p * slots:(p + 1) * slots], preferred_element_type=F32)
            obuf[pl.ds(p * 16 + q * RING, RING)] = value.astype(BF16).reshape(RING, rows, quarter)
        send(
            obuf.at[pl.ds((1 - c) * 16 + q * RING, RING)], pbuf.at[m, pl.ds(q * RING, RING)],
            s_send.at[m], sp_recv.at[m, number], partner,
        )

    def join(m, number):
        q = chunk(number)
        theirs = pl.ds(q * RING, RING)
        arrive(pbuf.at[m, theirs], sp_recv.at[m, number])
        mine = pl.ds(c * 16 + q * RING, RING)
        obuf[mine] = (obuf[mine].astype(F32) + pbuf[m, theirs].astype(F32)).astype(BF16)

    s_order = (f_far, f_dn, f_up, f)

    def to_ring(m, number):
        @pl.when(c == 0)
        def _():
            for kind, dg in ((2, 2), (0, 1), (1, -1)):
                spot = place(mod4(g + dg), s_order[number])
                send(obuf.at[spot], r2.at[m, kind, number], s_send.at[m], s2_recv.at[m, number, kind], device(0, dg))

        if number < RING - 1:
            @pl.when(c == 1)
            def _():
                kind, dg = ((2, 2), (1, -1), (0, 1))[number]
                for n in range(RING):
                    spot = 16 + place(mod4(g + dg), s_order[n])
                    send(obuf.at[spot], r2.at[m, kind, n], s_send.at[m], s2_recv.at[m, n, kind], device(0, dg))

    def second_ring(m, number):
        spot = c * 16 + place(g, s_order[number])
        total = obuf[spot].astype(F32)
        for kind in range(3):
            arrive(r2.at[m, kind, number], s2_recv.at[m, number, kind])
            total += r2[m, kind, number].astype(F32)
        if number == RING - 1:
            return total
        obuf[spot] = total.astype(BF16)
        send(
            obuf.at[spot], r3.at[m, number], s_send.at[m], s3_recv.at[m, number], device((2, -1, 1)[number], 0)
        )

    def finish(m):
        total = second_ring(m, RING - 1)
        for number in range(RING - 1):
            arrive(r3.at[m, number], s3_recv.at[m, number])
        spot = (m * 2 + c) * 16 + place(g, f)
        for h in range(2):
            value = xbuf[spot, part(h)].astype(F32) + total[h * (rows // 2):(h + 1) * (rows // 2)]
            for number in range(RING - 1):
                value += r3[m, number, part(h)].astype(F32)
            res[m, part(h)] = value.astype(BF16)

            @pl.when(s < segments - 1)
            def _():
                send(res.at[m, part(h)], xbuf.at[spot, part(h)], z_send.at[m], z_recv.at[m, h], above)

        out[m] = res[m]

    def project(m):
        down(m, 0)
        down(m, 1)
        join(m, 0)
        to_ring(m, 0)
        down(m, 2)
        join(m, 1)
        to_ring(m, 1)
        down(m, 3)
        join(m, 2)
        to_ring(m, 2)
        join(m, 3)
        to_ring(m, 3)

    def sent(m):
        arrive(xbuf.at[pl.ds(0, 28)], g_send.at[m])
        arrive(xbuf.at[pl.ds(0, 31)], s_send.at[m])

    @pl.when(s > 0)
    def _():
        set_up_routing()
        up_copy.wait()

    def one_batch(m, carry):
        start, turn, pass_on = gather_steps(m)
        start()
        turn()
        pass_on(0)

        @pl.when((s == 0) & (m == 0))
        def _():
            set_up_routing()
            up_copy.wait()

        up(m, 0)
        pass_on(1)
        pass_on(2)
        pass_on(3, (0, 1))
        up(m, 1)
        pass_on(3, (2,))
        up(m, 2)
        up(m, 3)

        @pl.when(m == 0)
        def _():
            down_copy.wait()

        project(m)
        for number in range(RING - 1):
            second_ring(m, number)
        finish(m)
        sent(m)
        return carry

    lax.fori_loop(0, batches, one_batch, 0)

    for step in range(7):
        arrive(meta, m_send.at[step])
    for step in range(3):
        arrive(gain, n_send.at[step])

    @pl.when(s < segments - 1)
    def _():
        for m in range(batches):
            arrive(res.at[m], z_send.at[m])


def on_device(inputs, norm_gain, up_weight, down_weight, routing, gates):
    batches, rows, quarter = inputs.shape
    width, hidden = up_weight.shape[2:]
    lanes = 2 * rows
    choice_rows = routing[0].astype(F32).transpose(0, 2, 1).reshape(2 * batches, rows)
    gate_rows = gates[0].transpose(0, 2, 1).reshape(2 * batches, rows)
    both = jnp.concatenate([choice_rows, gate_rows], axis=0)
    place = lax.rem(lax.axis_index("expert") // 2, 2)
    filled = jnp.concatenate([both, both], axis=1)
    meta = jnp.where(jnp.arange(lanes)[None, :] // rows == place, filled, 0.0)
    gain = jnp.broadcast_to(norm_gain, (8, quarter))
    slots = RING * CAP
    dma = pltpu.SemaphoreType.DMA
    vmem = pl.BlockSpec(memory_space=pltpu.VMEM)
    hbm = pl.BlockSpec(memory_space=pl.ANY)
    result = pl.pallas_call(
        relay_kernel,
        out_shape=jax.ShapeDtypeStruct((batches, rows, quarter), BF16),
        in_specs=[vmem, vmem, vmem, hbm, hbm],
        out_specs=vmem,
        scratch_shapes=[
            pltpu.VMEM((width, hidden), BF16),
            pltpu.VMEM((hidden, width), BF16),
            pltpu.VMEM((batches * 2 * 16, rows, quarter), BF16),
            pltpu.VMEM((2 * 16, rows, quarter), BF16),
            pltpu.VMEM((batches, 16, rows, quarter), BF16),
            pltpu.VMEM((batches, 3, RING, rows, quarter), BF16),
            pltpu.VMEM((batches, RING - 1, rows, quarter), BF16),
            pltpu.VMEM((batches, rows, quarter), BF16),
            pltpu.VMEM((2 * slots, quarter), BF16),
            pltpu.VMEM((2 * slots, hidden), F32),
            pltpu.VMEM((2 * slots, 1), F32),
            pltpu.VMEM((2 * slots, hidden), BF16),
            pltpu.VMEM((batches, 2, slots, RING * rows), BF16),
            pltpu.VMEM((batches, 2, RING * rows, slots), BF16),
            pltpu.VMEM((batches, 2 * slots, 1), F32),
            pltpu.VMEM((8, 8, lanes), F32),
            pltpu.VMEM((RING, 8, quarter), F32),
            pltpu.VMEM((16, RING * rows), BF16),
            dma((2,)),
            dma((8,)),
            dma((7,)),
            dma((4,)),
            dma((3,)),
            dma((batches,)),
            dma((batches, 2)),
            dma((batches, 3, 2)),
            dma((batches, RING, 3)),
            dma((batches, RING)),
            dma((batches,)),
            dma((batches,)),
            dma((batches, RING)),
            dma((batches, RING, 3)),
            dma((batches, RING - 1)),
            dma((batches,)),
        ],
        compiler_params=pltpu.CompilerParams(
            collective_id=0, has_side_effects=True, vmem_limit_bytes=67043328
        ),
    )(inputs, meta, gain, up_weight.reshape(width, hidden), down_weight.reshape(hidden, width))
    return result[None]


def solution(mesh):
    return jax.shard_map(
        on_device,
        mesh=mesh,
        in_specs=(
            P(None, "expert", "tensor"),
            P("segment", "tensor"),
            P("segment", "expert", None, "tensor"),
            P("segment", "expert", "tensor", None),
            P("segment", None, "expert", None),
            P("segment", None, "expert", None),
        ),
        out_specs=P("segment", None, "expert", "tensor"),
        check_vma=False,
    )
```

```python
import functools

import jax
import jax.numpy as jnp
from jax import lax
from jax.experimental import pallas as pl
from jax.experimental.pallas import tpu as pltpu
from jax.sharding import PartitionSpec as P

MESH = pl.DeviceIdType.MESH
RING = 4
CAP = 32
F32 = jnp.float32
BF16 = jnp.bfloat16


def relay_kernel(
    inp, choice, gate_in, gain, up_hbm, down_hbm, out,
    meta, wup, wdn, xbuf, obuf, pbuf, r2, r3, res, xg, acc, squares, hid, dmat, pmat, gslot, mbuf, gbuf, chosen,
    w_sem, m_send, m_recv, n_send, n_recv, z_send, z_recv,
    gf_recv, gg_recv, gp_recv, f_send, g_send, sp_recv, s2_recv, s3_recv, s_send,
):
    s = lax.axis_index("segment")
    e = lax.axis_index("expert")
    t = lax.axis_index("tensor")
    segments = lax.axis_size("segment")
    rows, quarter = inp.shape[1], inp.shape[2]
    width = quarter * RING
    hidden = wup.shape[1]
    batches = inp.shape[0]
    y = e // 2
    c = e - 2 * y
    f = t * (1 - c) + y * c
    g = y * (1 - c) + t * c

    def part(h):
        return pl.ds(h * (rows // 2), rows // 2)

    def mod4(v):
        return lax.rem(v + 8, 4)

    def device(df, dg):
        nf, ng = mod4(f + df), mod4(g + dg)
        nt = nf * (1 - c) + ng * c
        ny = ng * (1 - c) + nf * c
        return {"tensor": nt, "expert": 2 * ny + c}

    partner = {"expert": 2 * y + (1 - c)}
    above = {"segment": lax.rem(s + 1, segments)}
    below = {"segment": lax.rem(s + segments - 1, segments)}

    def place(gi, fi):
        q = fi * (1 - c) + gi * c
        yy = gi * (1 - c) + fi * c
        return q * RING + yy

    def send(src, dst, send_sem, recv_sem, where):
        pltpu.make_async_remote_copy(
            src_ref=src, dst_ref=dst, send_sem=send_sem, recv_sem=recv_sem, device_id=where, device_id_type=MESH
        ).start()

    def arrive(ref, sem):
        pltpu.make_async_copy(ref, ref, sem).wait()

    up_copy = pltpu.make_async_copy(up_hbm, wup, w_sem.at[0])
    down_copy = pltpu.make_async_copy(down_hbm, wdn, w_sem.at[1])
    up_copy.start()

    both = jnp.concatenate([choice[...].astype(F32), gate_in[...]], axis=0)
    both = jnp.concatenate([both, both], axis=1)
    lane = lax.broadcasted_iota(jnp.int32, both.shape, 1)
    meta[...] = jnp.where(lane // rows == lax.rem(y, 2), both, 0.0)

    barrier = pltpu.get_barrier_semaphore()
    for step in range(1, 8):
        pl.semaphore_signal(barrier, inc=1, device_id={"expert": lax.rem(e + step, 8)}, device_id_type=MESH)
    for step in range(1, RING):
        pl.semaphore_signal(barrier, inc=1, device_id={"tensor": lax.rem(t + step, RING)}, device_id_type=MESH)
    pl.semaphore_signal(barrier, inc=1, device_id=above, device_id_type=MESH)
    pl.semaphore_signal(barrier, inc=1, device_id=below, device_id_type=MESH)
    pl.semaphore_wait(barrier, 12)
    down_copy.start()

    @pl.when(s == 0)
    def _():
        for m in range(batches):
            for h in range(2):
                here = xbuf.at[(m * 2 + c) * 16 + place(g, f), part(h)]
                pltpu.make_async_copy(inp.at[m, part(h)], here, z_recv.at[m, h]).start()

    for step in range(1, 8):
        send(meta, mbuf.at[e], m_send.at[step - 1], m_recv.at[step - 1], {"expert": lax.rem(e + step, 8)})
    for step in range(1, RING):
        send(gain, gbuf.at[t], n_send.at[step - 1], n_recv.at[step - 1], {"tensor": lax.rem(t + step, RING)})
    own_meta = pltpu.make_async_copy(meta, mbuf.at[e], m_send.at[7])
    own_gain = pltpu.make_async_copy(gain, gbuf.at[t], n_send.at[3])
    own_meta.start()
    own_gain.start()

    slots = RING * CAP
    tokens = RING * rows
    f_far, f_dn, f_up = mod4(f + 2), mod4(f - 1), mod4(f + 1)
    g_far, g_dn, g_up = mod4(g + 2), mod4(g - 1), mod4(g + 1)

    def gather_steps(m):
        base = (m * 2 + c) * 16
        order = (f, f_dn, f_up, f_far)

        def to_partner(ref, number, g_number):
            group = number * (1 - c) + g_number * c
            send(ref, ref, g_send.at[m], gp_recv.at[m, group], partner)

        def spread(number):
            ref = xbuf.at[base + place(g, order[number])]
            for kind, dg in ((2, 2), (0, 1), (1, -1)):
                send(ref, ref, g_send.at[m], gg_recv.at[m, number, kind], device(0, dg))
            to_partner(ref, number, 0)

        def pass_on(number, kinds=(0, 1, 2)):
            for kind in kinds:
                ref = xbuf.at[base + place((g_dn, g_up, g_far)[kind], order[number])]
                arrive(ref, gg_recv.at[m, number, kind])
                to_partner(ref, number, 1 + kind)

        def start():
            for h in range(2):
                own = xbuf.at[base + place(g, f), part(h)]
                arrive(own, z_recv.at[m, h])
                for kind, df in ((2, 2), (0, 1), (1, -1)):
                    send(own, own, f_send.at[m], gf_recv.at[m, kind, h], device(df, 0))

        def leave():
            arrive(xbuf.at[pl.ds(0, 3)], f_send.at[m])
            spread(0)

        def turn():
            for number, fi in ((1, f_dn), (2, f_up), (3, f_far)):
                for h in range(2):
                    arrive(xbuf.at[base + place(g, fi), part(h)], gf_recv.at[m, number - 1, h])
                spread(number)

        return start, leave, turn, pass_on

    def set_up_routing():
        for step in range(7):
            arrive(meta, m_recv.at[step])
        for step in range(3):
            arrive(gain, n_recv.at[step])
        own_meta.wait()
        own_gain.wait()
        mine = e.astype(F32)
        row_i = lax.broadcasted_iota(jnp.int32, (tokens, tokens), 0)
        col_i = lax.broadcasted_iota(jnp.int32, (tokens, tokens), 1)
        earlier = ((row_i < col_i) & (row_i // rows == col_i // rows)).astype(BF16)
        slot_id = lax.broadcasted_iota(jnp.int32, (slots, tokens), 0).astype(F32)
        first_slot = (lax.broadcasted_iota(jnp.int32, (1, tokens), 1) // rows * CAP).astype(F32)
        for p in range(2):
            table = jnp.concatenate([mbuf[p] + mbuf[2 + p], mbuf[4 + p] + mbuf[6 + p]], axis=1)
            for mb in range(batches):
                hit0 = table[2 * mb:2 * mb + 1] == mine
                hit1 = table[2 * mb + 1:2 * mb + 2] == mine
                named = jnp.where(hit0 | hit1, 1.0, 0.0)
                chosen[...] = jnp.broadcast_to(named, chosen.shape).astype(BF16)
                before = jnp.dot(chosen[...], earlier, preferred_element_type=F32)[0:1]
                position = jnp.where(named > 0.0, before + first_slot, -1.0)
                gate = jnp.where(hit0, table[4 + 2 * mb:5 + 2 * mb], 0.0) + jnp.where(
                    hit1, table[5 + 2 * mb:6 + 2 * mb], 0.0
                )
                onehot = jnp.where(slot_id == position, 1.0, 0.0)
                dmat[mb, p] = onehot.astype(BF16)
                pmat[mb, p] = onehot.T.astype(BF16)
                gslot[mb, pl.ds(p * slots, slots)] = jnp.sum(onehot * gate, axis=1, keepdims=True)

    def up(m, number):
        q = mod4(t + (0, -1, 1, 2)[number])
        theirs = xbuf.at[pl.ds((m * 2 + 1 - c) * 16 + q * RING, RING)]
        arrive(theirs, gp_recv.at[m, number])
        for p in range(2):
            block = xbuf[pl.ds((m * 2 + p) * 16 + q * RING, RING)].reshape(tokens, quarter)
            picked = jnp.dot(dmat[m, p], block, preferred_element_type=F32)
            square = jnp.sum(picked * picked, axis=1, keepdims=True)
            mine = pl.ds(p * slots, slots)
            squares[mine] = square if number == 0 else squares[mine] + square
            xg[mine] = (picked * gbuf[q]).astype(BF16)
        step = hidden // 2
        deep = pl.ds(pl.multiple_of(q * quarter, quarter), quarter)
        for i in range(2):
            cols = pl.ds(i * step, step)
            v = jnp.dot(xg[...], wup[deep, cols], preferred_element_type=F32)
            if number > 0:
                v = v + acc[:, cols]
            if number < RING - 1:
                acc[:, cols] = v
            else:
                v = v * lax.rsqrt(squares[...] / width + 1e-05)
                hid[:, cols] = (v / (1.0 + jnp.exp(-v)) * gslot[m]).astype(BF16)

    def chunk(number):
        return mod4(t + (2, -1, 1, 0)[number])

    def down(m, number):
        q = chunk(number)
        cols = pl.ds(pl.multiple_of(q * quarter, quarter), quarter)
        part = jnp.dot(hid[...], wdn[:, cols], preferred_element_type=F32).astype(BF16)
        for p in range(2):
            value = jnp.dot(pmat[m, p], part[p * slots:(p + 1) * slots], preferred_element_type=F32)
            obuf[pl.ds(p * 16 + q * RING, RING)] = value.astype(BF16).reshape(RING, rows, quarter)
        send(
            obuf.at[pl.ds((1 - c) * 16 + q * RING, RING)], pbuf.at[m, pl.ds(q * RING, RING)],
            s_send.at[m], sp_recv.at[m, number], partner,
        )

    def join(m, number):
        q = chunk(number)
        theirs = pl.ds(q * RING, RING)
        arrive(pbuf.at[m, theirs], sp_recv.at[m, number])
        mine = pl.ds(c * 16 + q * RING, RING)
        obuf[mine] = (obuf[mine].astype(F32) + pbuf[m, theirs].astype(F32)).astype(BF16)

    s_order = (f_far, f_dn, f_up, f)

    def to_ring(m, number):
        @pl.when(c == 0)
        def _():
            for kind, dg in ((2, 2), (0, 1), (1, -1)):
                spot = place(mod4(g + dg), s_order[number])
                send(obuf.at[spot], r2.at[m, kind, number], s_send.at[m], s2_recv.at[m, number, kind], device(0, dg))

        if number < RING - 1:
            @pl.when(c == 1)
            def _():
                kind, dg = ((2, 2), (1, -1), (0, 1))[number]
                for n in range(RING):
                    spot = 16 + place(mod4(g + dg), s_order[n])
                    send(obuf.at[spot], r2.at[m, kind, n], s_send.at[m], s2_recv.at[m, n, kind], device(0, dg))

    def second_ring(m, number):
        spot = c * 16 + place(g, s_order[number])
        total = obuf[spot].astype(F32)
        for kind in range(3):
            arrive(r2.at[m, kind, number], s2_recv.at[m, number, kind])
            total += r2[m, kind, number].astype(F32)
        if number == RING - 1:
            return total
        obuf[spot] = total.astype(BF16)
        send(
            obuf.at[spot], r3.at[m, number], s_send.at[m], s3_recv.at[m, number], device((2, -1, 1)[number], 0)
        )

    def finish(m):
        total = second_ring(m, RING - 1)
        for number in range(RING - 1):
            arrive(r3.at[m, number], s3_recv.at[m, number])
        spot = (m * 2 + c) * 16 + place(g, f)
        for h in range(2):
            value = xbuf[spot, part(h)].astype(F32) + total[h * (rows // 2):(h + 1) * (rows // 2)]
            for number in range(RING - 1):
                value += r3[m, number, part(h)].astype(F32)
            res[m, part(h)] = value.astype(BF16)

            @pl.when(s < segments - 1)
            def _():
                send(res.at[m, part(h)], xbuf.at[spot, part(h)], z_send.at[m], z_recv.at[m, h], above)

        out[m] = res[m]

    def project(m):
        down(m, 0)
        down(m, 1)
        join(m, 0)
        to_ring(m, 0)
        down(m, 2)
        join(m, 1)
        to_ring(m, 1)
        down(m, 3)
        join(m, 2)
        to_ring(m, 2)
        join(m, 3)
        to_ring(m, 3)

    def sent(m):
        arrive(xbuf.at[pl.ds(0, 28)], g_send.at[m])
        arrive(xbuf.at[pl.ds(0, 31)], s_send.at[m])

    @pl.when(s > 0)
    def _():
        set_up_routing()
        up_copy.wait()

    steps = [gather_steps(m) for m in range(batches)]
    for m in range(batches):
        start, leave, turn, pass_on = steps[m]
        if m == 0:
            start()
        leave()
        turn()
        pass_on(0)
        if m == 0:
            @pl.when(s == 0)
            def _():
                set_up_routing()
                up_copy.wait()

        up(m, 0)
        pass_on(1)
        pass_on(2)
        pass_on(3, (0, 1))
        up(m, 1)
        pass_on(3, (2,))
        up(m, 2)
        up(m, 3)
        if m == 0:
            down_copy.wait()
        project(m)
        for number in range(RING - 1):
            second_ring(m, number)
        if m + 1 < batches:
            steps[m + 1][0]()
        finish(m)
        sent(m)

    for step in range(7):
        arrive(meta, m_send.at[step])
    for step in range(3):
        arrive(gain, n_send.at[step])

    @pl.when(s < segments - 1)
    def _():
        for m in range(batches):
            arrive(res.at[m], z_send.at[m])


def on_device(inputs, norm_gain, up_weight, down_weight, routing, gates):
    batches, rows, quarter = inputs.shape
    width, hidden = up_weight.shape[2:]
    choice = routing[0].transpose(0, 2, 1).reshape(2 * batches, rows)
    gate = gates[0].transpose(0, 2, 1).reshape(2 * batches, rows)
    slots = RING * CAP
    dma = pltpu.SemaphoreType.DMA
    vmem = pl.BlockSpec(memory_space=pltpu.VMEM)
    hbm = pl.BlockSpec(memory_space=pl.ANY)
    result = pl.pallas_call(
        relay_kernel,
        out_shape=jax.ShapeDtypeStruct((batches, rows, quarter), BF16),
        in_specs=[vmem, vmem, vmem, vmem, hbm, hbm],
        out_specs=vmem,
        scratch_shapes=[
            pltpu.VMEM((8, 2 * rows), F32),
            pltpu.VMEM((width, hidden), BF16),
            pltpu.VMEM((hidden, width), BF16),
            pltpu.VMEM((batches * 2 * 16, rows, quarter), BF16),
            pltpu.VMEM((2 * 16, rows, quarter), BF16),
            pltpu.VMEM((batches, 16, rows, quarter), BF16),
            pltpu.VMEM((batches, 3, RING, rows, quarter), BF16),
            pltpu.VMEM((batches, RING - 1, rows, quarter), BF16),
            pltpu.VMEM((batches, rows, quarter), BF16),
            pltpu.VMEM((2 * slots, quarter), BF16),
            pltpu.VMEM((2 * slots, hidden), F32),
            pltpu.VMEM((2 * slots, 1), F32),
            pltpu.VMEM((2 * slots, hidden), BF16),
            pltpu.VMEM((batches, 2, slots, RING * rows), BF16),
            pltpu.VMEM((batches, 2, RING * rows, slots), BF16),
            pltpu.VMEM((batches, 2 * slots, 1), F32),
            pltpu.VMEM((8, 8, 2 * rows), F32),
            pltpu.VMEM((RING, 1, quarter), F32),
            pltpu.VMEM((16, RING * rows), BF16),
            dma((2,)),
            dma((8,)),
            dma((7,)),
            dma((4,)),
            dma((3,)),
            dma((batches,)),
            dma((batches, 2)),
            dma((batches, 3, 2)),
            dma((batches, RING, 3)),
            dma((batches, RING)),
            dma((batches,)),
            dma((batches,)),
            dma((batches, RING)),
            dma((batches, RING, 3)),
            dma((batches, RING - 1)),
            dma((batches,)),
        ],
        compiler_params=pltpu.CompilerParams(
            collective_id=0, has_side_effects=True, vmem_limit_bytes=67043328
        ),
    )(inputs, choice, gate, norm_gain, up_weight.reshape(width, hidden), down_weight.reshape(hidden, width))
    return result[None]


def solution(mesh):
    return jax.shard_map(
        on_device,
        mesh=mesh,
        in_specs=(
            P(None, "expert", "tensor"),
            P("segment", "tensor"),
            P("segment", "expert", None, "tensor"),
            P("segment", "expert", "tensor", None),
            P("segment", None, "expert", None),
            P("segment", None, "expert", None),
        ),
        out_specs=P("segment", None, "expert", "tensor"),
        check_vma=False,
    )
```

```python
import functools

import jax
import jax.numpy as jnp
from jax import lax
from jax.experimental import pallas as pl
from jax.experimental.pallas import tpu as pltpu
from jax.sharding import PartitionSpec as P

MESH = pl.DeviceIdType.MESH
RING = 4
CAP = 32
F32 = jnp.float32
BF16 = jnp.bfloat16


def relay_kernel(
    inp, choice, gate_in, gain, up_hbm, down_hbm, out,
    meta, wup, wdn, xbuf, obuf, pbuf, r2, r3, res, xg, acc, squares, hid, dmat, pmat, gslot, mbuf, gbuf, chosen,
    w_sem, m_send, m_recv, n_send, n_recv, z_send, z_recv,
    gf_recv, gg_recv, gp_recv, f_send, g_send, sp_recv, s2_recv, s3_recv, s_send,
):
    s = lax.axis_index("segment")
    e = lax.axis_index("expert")
    t = lax.axis_index("tensor")
    segments = lax.axis_size("segment")
    rows, quarter = inp.shape[1], inp.shape[2]
    width = quarter * RING
    hidden = wup.shape[1]
    batches = inp.shape[0]
    y = e // 2
    c = e - 2 * y
    f = t * (1 - c) + y * c
    g = y * (1 - c) + t * c

    def part(h):
        return pl.ds(h * (rows // 2), rows // 2)

    def mod4(v):
        return lax.rem(v + 8, 4)

    def device(df, dg):
        nf, ng = mod4(f + df), mod4(g + dg)
        nt = nf * (1 - c) + ng * c
        ny = ng * (1 - c) + nf * c
        return {"tensor": nt, "expert": 2 * ny + c}

    partner = {"expert": 2 * y + (1 - c)}
    above = {"segment": lax.rem(s + 1, segments)}
    below = {"segment": lax.rem(s + segments - 1, segments)}

    def place(gi, fi):
        q = fi * (1 - c) + gi * c
        yy = gi * (1 - c) + fi * c
        return q * RING + yy

    def send(src, dst, send_sem, recv_sem, where):
        pltpu.make_async_remote_copy(
            src_ref=src, dst_ref=dst, send_sem=send_sem, recv_sem=recv_sem, device_id=where, device_id_type=MESH
        ).start()

    def arrive(ref, sem):
        pltpu.make_async_copy(ref, ref, sem).wait()

    up_copy = pltpu.make_async_copy(up_hbm, wup, w_sem.at[0])
    down_copy = pltpu.make_async_copy(down_hbm, wdn, w_sem.at[1])
    up_copy.start()

    @pl.when(s == 0)
    def _():
        for m in range(batches):
            for h in range(2):
                here = xbuf.at[(m * 2 + c) * 16 + place(g, f), part(h)]
                pltpu.make_async_copy(inp.at[m, part(h)], here, z_recv.at[m, h]).start()

    barrier = pltpu.get_barrier_semaphore()
    for step in range(1, 8):
        pl.semaphore_signal(barrier, inc=1, device_id={"expert": lax.rem(e + step, 8)}, device_id_type=MESH)
    for step in range(1, RING):
        pl.semaphore_signal(barrier, inc=1, device_id={"tensor": lax.rem(t + step, RING)}, device_id_type=MESH)
    pl.semaphore_signal(barrier, inc=1, device_id=above, device_id_type=MESH)
    pl.semaphore_signal(barrier, inc=1, device_id=below, device_id_type=MESH)

    both = jnp.concatenate([choice[...].astype(F32), gate_in[...]], axis=0)
    both = jnp.concatenate([both, both], axis=1)
    lane = lax.broadcasted_iota(jnp.int32, both.shape, 1)
    meta[...] = jnp.where(lane // rows == lax.rem(y, 2), both, 0.0)

    pl.semaphore_wait(barrier, 12)
    down_copy.start()

    for step in range(1, 8):
        send(meta, mbuf.at[e], m_send.at[step - 1], m_recv.at[step - 1], {"expert": lax.rem(e + step, 8)})
    for step in range(1, RING):
        send(gain, gbuf.at[t], n_send.at[step - 1], n_recv.at[step - 1], {"tensor": lax.rem(t + step, RING)})
    own_meta = pltpu.make_async_copy(meta, mbuf.at[e], m_send.at[7])
    own_gain = pltpu.make_async_copy(gain, gbuf.at[t], n_send.at[3])
    own_meta.start()
    own_gain.start()

    slots = RING * CAP
    tokens = RING * rows
    f_far, f_dn, f_up = mod4(f + 2), mod4(f - 1), mod4(f + 1)
    g_far, g_dn, g_up = mod4(g + 2), mod4(g - 1), mod4(g + 1)

    def gather_steps(m):
        base = (m * 2 + c) * 16
        order = (f, f_dn, f_up, f_far)

        def to_partner(ref, number, g_number):
            group = number * (1 - c) + g_number * c
            send(ref, ref, g_send.at[m], gp_recv.at[m, group], partner)

        def spread(number):
            ref = xbuf.at[base + place(g, order[number])]
            for kind, dg in ((2, 2), (0, 1), (1, -1)):
                send(ref, ref, g_send.at[m], gg_recv.at[m, number, kind], device(0, dg))
            to_partner(ref, number, 0)

        def pass_on(number, kinds=(0, 1, 2)):
            for kind in kinds:
                ref = xbuf.at[base + place((g_dn, g_up, g_far)[kind], order[number])]
                arrive(ref, gg_recv.at[m, number, kind])
                to_partner(ref, number, 1 + kind)

        def start():
            for h in range(2):
                own = xbuf.at[base + place(g, f), part(h)]
                arrive(own, z_recv.at[m, h])
                for kind, df in ((2, 2), (0, 1), (1, -1)):
                    send(own, own, f_send.at[m], gf_recv.at[m, kind, h], device(df, 0))

        def leave():
            arrive(xbuf.at[pl.ds(0, 3)], f_send.at[m])
            spread(0)

        def turn():
            for number, fi in ((1, f_dn), (2, f_up), (3, f_far)):
                for h in range(2):
                    arrive(xbuf.at[base + place(g, fi), part(h)], gf_recv.at[m, number - 1, h])
                spread(number)

        return start, leave, turn, pass_on

    def set_up_routing():
        for step in range(7):
            arrive(meta, m_recv.at[step])
        for step in range(3):
            arrive(gain, n_recv.at[step])
        own_meta.wait()
        own_gain.wait()
        mine = e.astype(F32)
        row_i = lax.broadcasted_iota(jnp.int32, (tokens, tokens), 0)
        col_i = lax.broadcasted_iota(jnp.int32, (tokens, tokens), 1)
        earlier = ((row_i < col_i) & (row_i // rows == col_i // rows)).astype(BF16)
        slot_id = lax.broadcasted_iota(jnp.int32, (slots, tokens), 0).astype(F32)
        first_slot = (lax.broadcasted_iota(jnp.int32, (1, tokens), 1) // rows * CAP).astype(F32)
        for p in range(2):
            table = jnp.concatenate([mbuf[p] + mbuf[2 + p], mbuf[4 + p] + mbuf[6 + p]], axis=1)
            for mb in range(batches):
                hit0 = table[2 * mb:2 * mb + 1] == mine
                hit1 = table[2 * mb + 1:2 * mb + 2] == mine
                named = jnp.where(hit0 | hit1, 1.0, 0.0)
                chosen[...] = jnp.broadcast_to(named, chosen.shape).astype(BF16)
                before = jnp.dot(chosen[...], earlier, preferred_element_type=F32)[0:1]
                position = jnp.where(named > 0.0, before + first_slot, -1.0)
                gate = jnp.where(hit0, table[4 + 2 * mb:5 + 2 * mb], 0.0) + jnp.where(
                    hit1, table[5 + 2 * mb:6 + 2 * mb], 0.0
                )
                onehot = jnp.where(slot_id == position, 1.0, 0.0)
                dmat[mb, p] = onehot.astype(BF16)
                pmat[mb, p] = onehot.T.astype(BF16)
                gslot[mb, pl.ds(p * slots, slots)] = jnp.sum(onehot * gate, axis=1, keepdims=True)

    def up(m, number):
        q = mod4(t + (0, -1, 1, 2)[number])
        theirs = xbuf.at[pl.ds((m * 2 + 1 - c) * 16 + q * RING, RING)]
        arrive(theirs, gp_recv.at[m, number])
        for p in range(2):
            block = xbuf[pl.ds((m * 2 + p) * 16 + q * RING, RING)].reshape(tokens, quarter)
            picked = jnp.dot(dmat[m, p], block, preferred_element_type=F32)
            square = jnp.sum(picked * picked, axis=1, keepdims=True)
            mine = pl.ds(p * slots, slots)
            squares[mine] = square if number == 0 else squares[mine] + square
            xg[mine] = (picked * gbuf[q]).astype(BF16)
        deep = pl.ds(pl.multiple_of(q * quarter, quarter), quarter)
        v = jnp.dot(xg[...], wup[deep, :], preferred_element_type=F32)
        if number > 0:
            v = v + acc[...]
        if number < RING - 1:
            acc[...] = v
        else:
            v = v * lax.rsqrt(squares[...] / width + 1e-05)
            hid[...] = (v / (1.0 + jnp.exp(-v)) * gslot[m]).astype(BF16)

    def chunk(number):
        return mod4(t + (2, -1, 1, 0)[number])

    def down(m, number):
        q = chunk(number)
        cols = pl.ds(pl.multiple_of(q * quarter, quarter), quarter)
        part = jnp.dot(hid[...], wdn[:, cols], preferred_element_type=F32).astype(BF16)
        for p in range(2):
            value = jnp.dot(pmat[m, p], part[p * slots:(p + 1) * slots], preferred_element_type=F32)
            obuf[pl.ds(p * 16 + q * RING, RING)] = value.astype(BF16).reshape(RING, rows, quarter)
        send(
            obuf.at[pl.ds((1 - c) * 16 + q * RING, RING)], pbuf.at[m, pl.ds(q * RING, RING)],
            s_send.at[m], sp_recv.at[m, number], partner,
        )

    def join(m, number):
        q = chunk(number)
        theirs = pl.ds(q * RING, RING)
        arrive(pbuf.at[m, theirs], sp_recv.at[m, number])
        mine = pl.ds(c * 16 + q * RING, RING)
        obuf[mine] = (obuf[mine].astype(F32) + pbuf[m, theirs].astype(F32)).astype(BF16)

    s_order = (f_far, f_dn, f_up, f)

    def to_ring(m, number):
        @pl.when(c == 0)
        def _():
            for kind, dg in ((2, 2), (0, 1), (1, -1)):
                spot = place(mod4(g + dg), s_order[number])
                send(obuf.at[spot], r2.at[m, kind, number], s_send.at[m], s2_recv.at[m, number, kind], device(0, dg))

        if number < RING - 1:
            @pl.when(c == 1)
            def _():
                kind, dg = ((2, 2), (1, -1), (0, 1))[number]
                for n in range(RING):
                    spot = 16 + place(mod4(g + dg), s_order[n])
                    send(obuf.at[spot], r2.at[m, kind, n], s_send.at[m], s2_recv.at[m, n, kind], device(0, dg))

    def second_ring(m, number):
        spot = c * 16 + place(g, s_order[number])
        total = obuf[spot].astype(F32)
        for kind in range(3):
            arrive(r2.at[m, kind, number], s2_recv.at[m, number, kind])
            total += r2[m, kind, number].astype(F32)
        if number == RING - 1:
            return total
        obuf[spot] = total.astype(BF16)
        send(
            obuf.at[spot], r3.at[m, number], s_send.at[m], s3_recv.at[m, number], device((2, -1, 1)[number], 0)
        )

    def finish(m):
        total = second_ring(m, RING - 1)
        for number in range(RING - 1):
            arrive(r3.at[m, number], s3_recv.at[m, number])
        spot = (m * 2 + c) * 16 + place(g, f)
        for h in range(2):
            value = xbuf[spot, part(h)].astype(F32) + total[h * (rows // 2):(h + 1) * (rows // 2)]
            for number in range(RING - 1):
                value += r3[m, number, part(h)].astype(F32)
            res[m, part(h)] = value.astype(BF16)

            @pl.when(s < segments - 1)
            def _():
                send(res.at[m, part(h)], xbuf.at[spot, part(h)], z_send.at[m], z_recv.at[m, h], above)

        out[m] = res[m]

    def project(m):
        down(m, 0)
        down(m, 1)
        join(m, 0)
        to_ring(m, 0)
        down(m, 2)
        join(m, 1)
        to_ring(m, 1)
        down(m, 3)
        join(m, 2)
        to_ring(m, 2)
        join(m, 3)
        to_ring(m, 3)

    def sent(m):
        arrive(xbuf.at[pl.ds(0, 28)], g_send.at[m])
        arrive(xbuf.at[pl.ds(0, 31)], s_send.at[m])

    @pl.when(s > 0)
    def _():
        set_up_routing()
        up_copy.wait()

    steps = [gather_steps(m) for m in range(batches)]
    for m in range(batches):
        start, leave, turn, pass_on = steps[m]
        if m == 0:
            start()
        leave()
        turn()
        pass_on(0)
        if m == 0:
            @pl.when(s == 0)
            def _():
                set_up_routing()
                up_copy.wait()

        up(m, 0)
        pass_on(1)
        pass_on(2)
        pass_on(3, (0, 1))
        up(m, 1)
        pass_on(3, (2,))
        up(m, 2)
        up(m, 3)
        if m == 0:
            down_copy.wait()
        project(m)
        for number in range(RING - 1):
            second_ring(m, number)
        if m + 1 < batches:
            steps[m + 1][0]()
        finish(m)
        sent(m)

    for step in range(7):
        arrive(meta, m_send.at[step])
    for step in range(3):
        arrive(gain, n_send.at[step])

    @pl.when(s < segments - 1)
    def _():
        for m in range(batches):
            arrive(res.at[m], z_send.at[m])


def on_device(inputs, norm_gain, up_weight, down_weight, routing, gates):
    batches, rows, quarter = inputs.shape
    width, hidden = up_weight.shape[2:]
    choice = routing[0].transpose(0, 2, 1).reshape(2 * batches, rows)
    gate = gates[0].transpose(0, 2, 1).reshape(2 * batches, rows)
    slots = RING * CAP
    dma = pltpu.SemaphoreType.DMA
    vmem = pl.BlockSpec(memory_space=pltpu.VMEM)
    hbm = pl.BlockSpec(memory_space=pl.ANY)
    result = pl.pallas_call(
        relay_kernel,
        out_shape=jax.ShapeDtypeStruct((batches, rows, quarter), BF16),
        in_specs=[vmem, vmem, vmem, vmem, hbm, hbm],
        out_specs=vmem,
        scratch_shapes=[
            pltpu.VMEM((8, 2 * rows), F32),
            pltpu.VMEM((width, hidden), BF16),
            pltpu.VMEM((hidden, width), BF16),
            pltpu.VMEM((batches * 2 * 16, rows, quarter), BF16),
            pltpu.VMEM((2 * 16, rows, quarter), BF16),
            pltpu.VMEM((batches, 16, rows, quarter), BF16),
            pltpu.VMEM((batches, 3, RING, rows, quarter), BF16),
            pltpu.VMEM((batches, RING - 1, rows, quarter), BF16),
            pltpu.VMEM((batches, rows, quarter), BF16),
            pltpu.VMEM((2 * slots, quarter), BF16),
            pltpu.VMEM((2 * slots, hidden), F32),
            pltpu.VMEM((2 * slots, 1), F32),
            pltpu.VMEM((2 * slots, hidden), BF16),
            pltpu.VMEM((batches, 2, slots, RING * rows), BF16),
            pltpu.VMEM((batches, 2, RING * rows, slots), BF16),
            pltpu.VMEM((batches, 2 * slots, 1), F32),
            pltpu.VMEM((8, 8, 2 * rows), F32),
            pltpu.VMEM((RING, 1, quarter), F32),
            pltpu.VMEM((16, RING * rows), BF16),
            dma((2,)),
            dma((8,)),
            dma((7,)),
            dma((4,)),
            dma((3,)),
            dma((batches,)),
            dma((batches, 2)),
            dma((batches, 3, 2)),
            dma((batches, RING, 3)),
            dma((batches, RING)),
            dma((batches,)),
            dma((batches,)),
            dma((batches, RING)),
            dma((batches, RING, 3)),
            dma((batches, RING - 1)),
            dma((batches,)),
        ],
        compiler_params=pltpu.CompilerParams(
            collective_id=0, has_side_effects=True, vmem_limit_bytes=67043328
        ),
    )(inputs, choice, gate, norm_gain, up_weight.reshape(width, hidden), down_weight.reshape(hidden, width))
    return result[None]


def solution(mesh):
    return jax.shard_map(
        on_device,
        mesh=mesh,
        in_specs=(
            P(None, "expert", "tensor"),
            P("segment", "tensor"),
            P("segment", "expert", None, "tensor"),
            P("segment", "expert", "tensor", None),
            P("segment", None, "expert", None),
            P("segment", None, "expert", None),
        ),
        out_specs=P("segment", None, "expert", "tensor"),
        check_vma=False,
    )
```
